32 devices in a mesh: row: 8 (over z, y), col: 4 (over x, core).
Axes of the slice: x: 2, y: 2, z: 4, core: 2. Of those that a mesh axis runs over, the one named last changes fastest.
Arguments:
- left_blocks: bfloat16 [2, 128, 512, 128], P(None, 'row', 'col'), may hold values from -0.1875 to 0.1875
- right_blocks: bfloat16 [128, 512, 128], P('row', 'col'), may hold values from -6 to 6
- left_index: int32 [2, 512, 32], P(None, 'row', 'col'), may hold values from 0 to 16, as said below
- right_index: int32 [2, 512, 32], P(None, 'row', 'col'), may hold values from 0 to 15
Outputs:
- out_blocks: bfloat16 [512, 512, 128], P('row', 'col')
The draws below stay inside these ranges and needn't reach their ends.
Inputs may be any that keep to these rules, and one draw needn't show every extreme that they name: `left_index`: the value 16 marks a padded pair that adds nothing; in every step and on every device each result block has 1 to 8 live pairs.
All inputs are finite; a program needn't handle non-finite values.
Results may differ from the reference program's by a relative error of at most 0.001.
Values may be sent and summed in bfloat16 or wider, within the bound.
No kernel may reach another device: no remote copies, remote signals or barrier semaphores. Data moves between devices by JAX's collectives and lax.ppermute only.
A program may use at most 128 MiB of HBM per device.

```python
import jax
import jax.numpy as jnp
from jax import lax

BLK = 128
NZ = 16
SLOTS = 64
GROUP = 8
STEPS = 2
HELD = 2
N_ROW = 8
N_COL = 4


def draw_left_index(key, part):
    count_key = jax.random.fold_in(key, 11)
    value_key = jax.random.fold_in(key, 12)
    counts = jax.random.randint(count_key, (STEPS, SLOTS * N_ROW, N_COL), 1, GROUP + 1)
    slot_of = jnp.arange(SLOTS * N_ROW) % SLOTS
    counts = jnp.where(slot_of[None, :, None] == 0, 1, counts)
    counts = jnp.repeat(counts, GROUP, axis=2)
    position = jnp.arange(GROUP * N_COL) % GROUP
    values = jax.random.randint(value_key, (STEPS, SLOTS * N_ROW, GROUP * N_COL), 0, NZ)
    return jnp.where(position[None, None, :] < counts, values, NZ).astype(jnp.int32)


def touch_ends(drawn, stream_key, smallest, top_value):
    dims = drawn.shape
    spot = [jax.random.randint(jax.random.fold_in(stream_key, axis), (), 0, dims[axis]) for axis in range(len(dims))]
    drawn = drawn.at[tuple(spot)].set(smallest)
    longest = dims.index(max(dims))
    spot[longest] = (spot[longest] + 1) % dims[longest]
    return drawn.at[tuple(spot)].set(top_value)


def block_scale(stream_key, dims, shards, least, top_value):
    level = 1.0
    for dim, shards_of in shards:
        draws = jax.random.uniform(jax.random.fold_in(jax.random.fold_in(stream_key, 6), dim), (shards_of,), jnp.float32, least / len(shards), top_value / len(shards))
        level = level * jnp.repeat(jnp.exp(draws), dims[dim] // shards_of).reshape((-1,) + (1,) * (len(dims) - 1 - dim))
    return level


def gaussian(own_key, shape, width, bound, split=(), kind=jnp.bfloat16):
    drawn = jax.random.normal(own_key, shape, jnp.float32) * width
    if len(split) > 0:
        drawn = block_scale(own_key, shape, split, -0.22, 0.18) * drawn
    return jnp.clip(drawn, min=-bound, max=bound).astype(kind)


def setup_inputs(seed: int = 0) -> dict:
    streams_of = jax.random.split(jax.random.key(seed), 5)
    left_blocks = gaussian(streams_of[0], (HELD, NZ * N_ROW, BLK * N_COL, BLK), (BLK * GROUP) ** -0.5, 0.1875, ((1, 8), (2, 4)))
    right_blocks = gaussian(streams_of[1], (NZ * N_ROW, BLK * N_COL, BLK), 1.0, 6.0, ((0, 8), (1, 4)))
    left_index = draw_left_index(jax.random.fold_in(streams_of[4], 71), 0)
    right_index = touch_ends(jax.random.randint(streams_of[3], (STEPS, SLOTS * N_ROW, GROUP * N_COL), 0, NZ), jax.random.fold_in(streams_of[3], 1), 0, NZ - 1).astype(jnp.int32)
    return dict(left_blocks=left_blocks, right_blocks=right_blocks, left_index=left_index, right_index=right_index)


def reference(left_blocks, right_blocks, left_index, right_index):
    left_view = left_blocks.reshape(HELD, N_ROW, NZ, N_COL, BLK, BLK)
    right_view = right_blocks.reshape(N_ROW, NZ, N_COL, BLK, BLK)
    left_pairs = left_index.reshape(STEPS, N_ROW, SLOTS, N_COL, GROUP)
    right_pairs = right_index.reshape(STEPS, N_ROW, SLOTS, N_COL, GROUP)
    zero_block = jnp.zeros((1, BLK, BLK), jnp.float32)

    def per_device(device):
        row_at = device // N_COL
        col_at = device % N_COL
        accumulated = jnp.zeros((SLOTS, BLK, BLK), jnp.float32)
        for step_index in range(STEPS):
            panel_index = (row_at + step_index) % N_ROW
            own_slot = panel_index // N_COL
            panel_col = panel_index % N_COL
            left_panel = left_view[own_slot, row_at, :, panel_col].astype(jnp.float32)
            left_panel = jnp.concatenate([left_panel, zero_block], axis=0)
            right_panel = right_view[panel_index, :, col_at].astype(jnp.float32)
            left_rows = left_pairs[step_index, row_at, :, col_at]
            right_rows = right_pairs[step_index, row_at, :, col_at]
            left_tiles = jnp.take(left_panel, left_rows, axis=0)
            right_tiles = jnp.take(right_panel, right_rows, axis=0)
            accumulated = accumulated + jnp.einsum("sgij,sgjl->sil", left_tiles, right_tiles)
        return accumulated.astype(jnp.bfloat16)

    stacked = lax.map(per_device, jnp.arange(N_ROW * N_COL, dtype=jnp.int32))
    stacked = stacked.reshape(N_ROW, N_COL, SLOTS, BLK, BLK).transpose(0, 2, 1, 3, 4)
    return stacked.reshape(N_ROW * SLOTS, N_COL * BLK, BLK)
```

```python
import functools

import jax
import jax.numpy as jnp
from jax import lax
from jax.experimental import pallas as pl
from jax.experimental.pallas import tpu as pltpu
from jax.sharding import PartitionSpec as P


def spread_pairs(row_count, col_count, bit):
    pairs = []
    for r in range(row_count):
        held = {r % col_count, (r + 1) % col_count}
        b = col_count // 2
        while b > bit:
            held |= {c ^ b for c in held}
            b //= 2
        pairs += [(r * col_count + c, r * col_count + (c ^ bit)) for c in sorted(held)]
    return pairs


def pair_kernel(step, per_block, unroll, has_sum, left_rows, right_rows, first, second, right, *rest):
    if has_sum:
        summed, out, panel = rest
    else:
        out, panel = rest
        summed = None
    stored = first.shape[0]

    @pl.when(pl.program_id(0) == 0)
    def _():
        same = (lax.axis_index("row") + lax.axis_index("col") + step) % 2 == 0

        @pl.when(same)
        def _():
            panel[pl.ds(0, stored)] = first[...]

        @pl.when(jnp.logical_not(same))
        def _():
            panel[pl.ds(0, stored)] = second[...]

        panel[stored] = jnp.zeros(panel.shape[1:], panel.dtype)

    base = pl.program_id(0) * per_block
    group = left_rows.shape[1]

    def one(j, carry):
        t = base + j
        a = jnp.concatenate([panel[left_rows[step, g, t]] for g in range(group)], axis=1)
        b = jnp.concatenate([right[right_rows[step, g, t]] for g in range(group)], axis=0)
        x = jnp.dot(a, b, preferred_element_type=jnp.float32)
        if summed is not None:
            x = x + summed[j]
        out[j] = x.astype(out.dtype)
        return carry

    lax.fori_loop(0, per_block, one, 0, unroll=unroll)


def pair_sums(step, left_rows, right_rows, first, second, right, summed, dtype):
    stored, block, _ = right.shape
    group, slots = left_rows.shape[1:]
    per_block = min(slots, 16)
    whole = pl.BlockSpec(right.shape, lambda i: (0, 0, 0))
    tile = pl.BlockSpec((per_block, block, block), lambda i: (i, 0, 0))
    index = pl.BlockSpec(memory_space=pltpu.SMEM)
    operands = (left_rows, right_rows, first, second, right)
    specs = [index, index, whole, whole, whole]
    if summed is not None:
        operands += (summed,)
        specs.append(tile)
    return pl.pallas_call(
        functools.partial(pair_kernel, step, per_block, 8, summed is not None),
        grid=(slots // per_block,),
        out_shape=jax.ShapeDtypeStruct((slots, block, block), dtype),
        in_specs=specs,
        out_specs=tile,
        scratch_shapes=[pltpu.VMEM((stored + 1, block, block), right.dtype)],
        cost_estimate=pl.CostEstimate(
            flops=4 * slots * group * block**3, bytes_accessed=8 << 20, transcendentals=0
        ),
        name="pairs",
    )(*operands)


def per_device(left_blocks, right_blocks, left_index, right_index):
    row_count, col_count = lax.axis_size("row"), lax.axis_size("col")
    row_at, col_at = lax.axis_index("row"), lax.axis_index("col")
    left_rows = left_index.transpose(0, 2, 1)
    right_rows = right_index.transpose(0, 2, 1)

    moved_right = lax.ppermute(
        right_blocks, "row", [(r, (r - 1) % row_count) for r in range(row_count)]
    )
    ahead = (row_at + col_at) % 2
    slot = ((row_at + ahead) % row_count) // col_count
    current = lax.dynamic_index_in_dim(left_blocks, slot, 0, keepdims=False)
    bit = col_count // 2
    away = col_at ^ ((row_at + ahead) % col_count)
    while bit > 1:
        received = lax.ppermute(current, ("row", "col"), spread_pairs(row_count, col_count, bit))
        current = jnp.where((away & bit) != 0, received, current)
        bit //= 2
    other = lax.ppermute(current, "col", [(c, c ^ 1) for c in range(col_count)])
    partial = pair_sums(0, left_rows, right_rows, current, other, right_blocks, None, jnp.float32)
    return pair_sums(1, left_rows, right_rows, current, other, moved_right, partial, jnp.bfloat16)


def solution(mesh):
    return jax.shard_map(
        per_device,
        mesh=mesh,
        in_specs=(
            P(None, "row", "col", None),
            P("row", "col", None),
            P(None, "row", "col"),
            P(None, "row", "col"),
        ),
        out_specs=P("row", "col", None),
        check_vma=False,
    )
```

```python
import functools

import jax
import jax.numpy as jnp
from jax import lax
from jax.experimental import pallas as pl
from jax.experimental.pallas import tpu as pltpu
from jax.sharding import PartitionSpec as P


VMEM = pl.BlockSpec(memory_space=pltpu.VMEM)
SMEM = pl.BlockSpec(memory_space=pltpu.SMEM)
HBM = pl.BlockSpec(memory_space=pltpu.HBM)


def in_vmem(x):
    return pltpu.with_memory_space_constraint(x, pltpu.VMEM)


def holders(row, col_count, ahead, bit):
    held = {(row + ahead) % col_count}
    step = col_count // 2
    while step > bit:
        held |= {c ^ step for c in held}
        step //= 2
    return held


def full_pairs(row_count, col_count, wanted):
    pairs = []
    for row in range(row_count):
        pair_of = dict(wanted(row))
        sources = [c for c in range(col_count) if c not in pair_of]
        targets = set(range(col_count)) - set(pair_of.values())
        for c in list(sources):
            if c ^ 1 in targets:
                pair_of[c] = c ^ 1
                targets.remove(c ^ 1)
                sources.remove(c)
        pair_of.update(zip(sources, sorted(targets)))
        pairs += [(row * col_count + c, row * col_count + to) for c, to in sorted(pair_of.items())]
    return pairs


def place():
    row, col = lax.axis_index("row"), lax.axis_index("col")
    ahead = (row + col) % 2
    away = col ^ ((row + ahead) % lax.axis_size("col"))
    return row % 2, ahead, away


def fetch_kernel(left, right, out, right_out, sem):
    row_count, col_count = lax.axis_size("row"), lax.axis_size("col")
    row = lax.axis_index("row")
    ahead = (row + lax.axis_index("col")) % 2
    slot = ((row + ahead) % row_count) // col_count
    copies = [
        pltpu.make_async_copy(left.at[slot], out, sem.at[0]),
        pltpu.make_async_copy(right, right_out, sem.at[1]),
    ]
    for copy in copies:
        copy.start()
    for copy in copies:
        copy.wait()


def fetch(left_blocks, right_blocks):
    return pl.pallas_call(
        fetch_kernel,
        out_shape=(
            jax.ShapeDtypeStruct(left_blocks.shape[1:], left_blocks.dtype),
            jax.ShapeDtypeStruct(right_blocks.shape, right_blocks.dtype),
        ),
        in_specs=[HBM, HBM],
        out_specs=(VMEM, VMEM),
        scratch_shapes=[pltpu.SemaphoreType.DMA((2,))],
        compiler_params=pltpu.CompilerParams(vmem_limit_bytes=4 << 20),
        name="fetch",
    )(
        pltpu.with_memory_space_constraint(left_blocks, pltpu.HBM),
        pltpu.with_memory_space_constraint(right_blocks, pltpu.HBM),
    )


def merge_kernel(bit, split, base, received, current, kept):
    odd, ahead, away = place()
    take = (away & bit) != 0
    if split:
        take = jnp.logical_and(take, jnp.logical_or(odd == 1, ahead == 0))

    @pl.when(take)
    def _():
        current[...] = received[...]

    @pl.when(jnp.logical_not(take))
    def _():
        current[...] = base[...]

    kept[...] = base[...]


def merge(bit, split, base, received):
    shape = jax.ShapeDtypeStruct(base.shape, base.dtype)
    return pl.pallas_call(
        functools.partial(merge_kernel, bit, split),
        out_shape=(shape, shape),
        in_specs=[VMEM, VMEM],
        out_specs=(VMEM, VMEM),
        compiler_params=pltpu.CompilerParams(vmem_limit_bytes=4 << 20),
        name="merge",
    )(in_vmem(base), in_vmem(received))


def products(panel, right, out):
    stored, block, _ = panel.shape
    rows = panel[...].reshape(stored * block, block)

    def one(q, carry):
        pair = jnp.concatenate([right[2 * q], right[2 * q + 1]], axis=1)
        x = jnp.dot(rows, pair, preferred_element_type=jnp.float32)
        base = 2 * q * stored
        out[pl.ds(base, stored)] = x[:, :block].reshape(stored, block, block)
        out[pl.ds(base + stored, stored)] = x[:, block:].reshape(stored, block, block)
        return carry

    lax.fori_loop(0, right.shape[0] // 2, one, 0, unroll=8)


def gathered(index, step, t, table):
    x = table[index[step, 0, t]]
    for g in range(1, index.shape[1]):
        x = x + table[index[step, g, t]]
    return x


def first_products_kernel(current, other, right, out, panel):
    _, ahead, _ = place()

    @pl.when(ahead == 0)
    def _():
        panel[...] = current[...]

    @pl.when(ahead == 1)
    def _():
        panel[...] = other[...]

    products(panel, right, out)
    out[out.shape[0] - 1] = jnp.zeros(out.shape[1:], out.dtype)


def first_sums_kernel(index, table, out):
    def one(t, carry):
        out[t] = gathered(index, 0, t, table)
        return carry

    lax.fori_loop(0, out.shape[0], one, 0, unroll=8)


def second_kernel(per_block, index, current, other, crossed, passed, right, summed, out, panel, table):
    @pl.when(pl.program_id(0) == 0)
    def _():
        odd, ahead, away = place()
        late = jnp.logical_and(odd == 0, (away & 2) != 0)
        prompt = jnp.logical_not(late)

        @pl.when(jnp.logical_and(late, ahead == 0))
        def _():
            panel[...] = passed[...]

        @pl.when(jnp.logical_and(late, ahead == 1))
        def _():
            panel[...] = crossed[...]

        @pl.when(jnp.logical_and(prompt, ahead == 0))
        def _():
            panel[...] = other[...]

        @pl.when(jnp.logical_and(prompt, ahead == 1))
        def _():
            panel[...] = current[...]

        products(panel, right, table)
        table[table.shape[0] - 1] = jnp.zeros(table.shape[1:], table.dtype)

    base = pl.program_id(0) * per_block

    def one(j, carry):
        t = base + j
        out[j] = (summed[t] + gathered(index, 1, t, table)).astype(out.dtype)
        return carry

    lax.fori_loop(0, per_block, one, 0, unroll=8)


def cost(flops, bytes_accessed):
    return pl.CostEstimate(flops=flops, bytes_accessed=bytes_accessed, transcendentals=0)


def both_steps(left_blocks, right_blocks, left_index, right_index):
    row_count, col_count = lax.axis_size("row"), lax.axis_size("col")
    stored, block, _ = right_blocks.shape
    slots = left_index.shape[1]
    entries = stored * stored + 1
    both = ("row", "col")

    moved_right = lax.ppermute(
        right_blocks, "row", [(r, (r - 1) % row_count) for r in range(row_count)]
    )
    left_at, right_at = left_index.transpose(0, 2, 1), right_index.transpose(0, 2, 1)
    index = jnp.where(left_at < stored, right_at * stored + left_at, stored * stored)

    base, own_right = fetch(left_blocks, right_blocks)
    bit = col_count // 2
    while bit > 2:
        pairs = full_pairs(row_count, col_count, lambda row: [
            (c, c ^ bit) for c in holders(row, col_count, 0, bit) | holders(row, col_count, 1, bit)
        ])
        base, _ = merge(bit, False, base, lax.ppermute(base, both, pairs))
        bit //= 2
    early = full_pairs(row_count, col_count, lambda row: [
        (c, c ^ 2)
        for ahead in range(1 + row % 2)
        for c in holders(row, col_count, ahead, 2)
    ])
    late = full_pairs(row_count, col_count, lambda row: [
        (c, c ^ 2) for c in holders(row, col_count, 1, 2) if row % 2 == 0
    ])
    across = [(c, c ^ 1) for c in range(col_count)]
    received = lax.ppermute(base, both, early)
    current, kept = merge(2, True, base, received)
    crossed = lax.ppermute(kept, both, late)
    other = lax.ppermute(current, "col", across)
    passed = lax.ppermute(crossed, "col", across)

    flops = 4 * stored * stored * block**3
    table = pl.pallas_call(
        first_products_kernel,
        out_shape=jax.ShapeDtypeStruct((entries, block, block), jnp.float32),
        in_specs=[VMEM] * 3,
        out_specs=VMEM,
        scratch_shapes=[pltpu.VMEM(right_blocks.shape, right_blocks.dtype)],
        compiler_params=pltpu.CompilerParams(vmem_limit_bytes=22 << 20),
        cost_estimate=cost(flops, 4 << 20),
        name="products",
    )(in_vmem(current), in_vmem(other), in_vmem(own_right))
    summed = pl.pallas_call(
        first_sums_kernel,
        out_shape=jax.ShapeDtypeStruct((slots, block, block), jnp.float32),
        in_specs=[SMEM, VMEM],
        out_specs=VMEM,
        compiler_params=pltpu.CompilerParams(vmem_limit_bytes=8 << 20),
        cost_estimate=cost(flops, 4 << 20),
        name="sums",
    )(index, in_vmem(table))
    per_block = min(slots, 16)
    return pl.pallas_call(
        functools.partial(second_kernel, per_block),
        grid=(slots // per_block,),
        out_shape=jax.ShapeDtypeStruct((slots, block, block), jnp.bfloat16),
        in_specs=[SMEM] + [VMEM] * 6,
        out_specs=pl.BlockSpec((per_block, block, block), lambda i: (i, 0, 0)),
        scratch_shapes=[
            pltpu.VMEM(right_blocks.shape, right_blocks.dtype),
            pltpu.VMEM((entries, block, block), jnp.float32),
        ],
        compiler_params=pltpu.CompilerParams(vmem_limit_bytes=22 << 20),
        cost_estimate=cost(2 * flops, 4 << 20),
        name="second",
    )(index, *map(in_vmem, (current, other, crossed, passed, moved_right, summed)))


def solution(mesh):
    return jax.shard_map(
        both_steps,
        mesh=mesh,
        in_specs=(
            P(None, "row", "col", None),
            P("row", "col", None),
            P(None, "row", "col"),
            P(None, "row", "col"),
        ),
        out_specs=P("row", "col", None),
        check_vma=False,
    )
```

```python
import functools

import jax
import jax.numpy as jnp
from jax import lax
from jax.experimental import pallas as pl
from jax.experimental.pallas import tpu as pltpu
from jax.sharding import PartitionSpec as P


VMEM = pl.BlockSpec(memory_space=pltpu.VMEM)
HBM = pl.BlockSpec(memory_space=pltpu.HBM)


def in_vmem(x):
    return pltpu.with_memory_space_constraint(x, pltpu.VMEM)


def holders(row, col_count, ahead, bit):
    held = {(row + ahead) % col_count}
    step = col_count // 2
    while step > bit:
        held |= {c ^ step for c in held}
        step //= 2
    return held


def full_pairs(row_count, col_count, wanted):
    pairs = []
    for row in range(row_count):
        pair_of = dict(wanted(row))
        sources = [c for c in range(col_count) if c not in pair_of]
        targets = set(range(col_count)) - set(pair_of.values())
        for c in list(sources):
            if c ^ 1 in targets:
                pair_of[c] = c ^ 1
                targets.remove(c ^ 1)
                sources.remove(c)
        pair_of.update(zip(sources, sorted(targets)))
        pairs += [(row * col_count + c, row * col_count + to) for c, to in sorted(pair_of.items())]
    return pairs


def place():
    row, col = lax.axis_index("row"), lax.axis_index("col")
    return row % 2, (col ^ row) % 4, (col ^ (row + 1)) % 4


def plan_step(left_at, right_at, stored):
    group, slots = left_at.shape
    dead = stored * stored
    index = jnp.where(left_at < stored, right_at * stored + left_at, dead)
    rows = [index[g : g + 1] for g in range(group)]
    for turn in range(group):
        for g in range(turn % 2, group - 1, 2):
            rows[g], rows[g + 1] = jnp.minimum(*rows[g : g + 2]), jnp.maximum(*rows[g : g + 2])
    live = sum((row < dead).astype(jnp.float32) for row in rows)
    at_row = lax.broadcasted_iota(jnp.int32, (slots, slots), 0).astype(jnp.float32)
    at_col = lax.broadcasted_iota(jnp.int32, (slots, slots), 1).astype(jnp.float32)
    slot = at_col[:1]
    key = live * slots - slot
    column = jnp.sum(jnp.where(at_row == at_col, key, 0.0), axis=1, keepdims=True)
    rank = jnp.sum((key > column).astype(jnp.float32), axis=1, keepdims=True)
    pick = (rank == at_col).astype(jnp.float32)
    data = jnp.concatenate([row.astype(jnp.float32) for row in rows] + [live, slot], axis=0)
    sorted_data = jnp.dot(
        data, pick, precision=lax.Precision.HIGHEST, preferred_element_type=jnp.float32
    )
    return (sorted_data + 0.5).astype(jnp.int32)


def fetch_kernel(left, right, left_at, right_at, own, low, high, plan, at, sem):
    row_count, col_count = lax.axis_size("row"), lax.axis_size("col")
    row = lax.axis_index("row")
    ahead = (row + lax.axis_index("col")) % 2
    slot = ((row + ahead) % row_count) // col_count
    split = low.shape[0]
    copies = [
        pltpu.make_async_copy(left_at, at.at[0], sem.at[0]),
        pltpu.make_async_copy(right_at, at.at[1], sem.at[1]),
        pltpu.make_async_copy(left.at[slot], own, sem.at[2]),
        pltpu.make_async_copy(right.at[pl.ds(0, split)], low, sem.at[3]),
        pltpu.make_async_copy(right.at[pl.ds(split, high.shape[0])], high, sem.at[4]),
    ]
    for copy in copies:
        copy.start()
    for copy in copies[:2]:
        copy.wait()
    for step in range(plan.shape[0]):
        plan[step] = plan_step(at[0, step], at[1, step], own.shape[0])
    for copy in copies[2:]:
        copy.wait()


def fetch(left_blocks, right_blocks, left_at, right_at, split):
    stored, *block = right_blocks.shape
    steps, group, slots = left_at.shape
    return pl.pallas_call(
        fetch_kernel,
        out_shape=tuple(
            jax.ShapeDtypeStruct((count, *block), right_blocks.dtype)
            for count in (stored, split, stored - split)
        ) + (jax.ShapeDtypeStruct((steps, group + 2, slots), jnp.int32),),
        in_specs=[HBM] * 4,
        out_specs=(VMEM,) * 4,
        scratch_shapes=[
            pltpu.VMEM((2, steps, group, slots), jnp.int32),
            pltpu.SemaphoreType.DMA((5,)),
        ],
        compiler_params=pltpu.CompilerParams(vmem_limit_bytes=4 << 20),
        name="fetch",
    )(*(pltpu.with_memory_space_constraint(x, pltpu.HBM)
        for x in (left_blocks, right_blocks, left_at, right_at)))


def merge_kernel(bit, base, received, out):
    row, col = lax.axis_index("row"), lax.axis_index("col")
    away = col ^ ((row + (row + col) % 2) % lax.axis_size("col"))
    take = (away & bit) != 0

    @pl.when(take)
    def _():
        out[...] = received[...]

    @pl.when(jnp.logical_not(take))
    def _():
        out[...] = base[...]


def merge(bit, base, received):
    return pl.pallas_call(
        functools.partial(merge_kernel, bit),
        out_shape=jax.ShapeDtypeStruct(base.shape, base.dtype),
        in_specs=[VMEM, VMEM],
        out_specs=VMEM,
        compiler_params=pltpu.CompilerParams(vmem_limit_bytes=4 << 20),
        name="merge",
    )(in_vmem(base), in_vmem(received))


def choose(panel, options):
    for condition, array in options:
        @pl.when(condition)
        def _():
            panel[...] = array[...]


def products(panel, right, out, first):
    stored, block, _ = panel.shape
    rows = panel[...].reshape(stored * block, block)
    for q in range(right.shape[0] // 2):
        pair = jnp.concatenate([right[2 * q], right[2 * q + 1]], axis=1)
        x = jnp.dot(rows, pair, preferred_element_type=jnp.float32)
        base = (first + 2 * q) * stored
        out[pl.ds(base, stored)] = x[:, :block].reshape(stored, block, block)
        out[pl.ds(base + stored, stored)] = x[:, block:].reshape(stored, block, block)


def add_up(plan, step, table, per_turn, put):
    group = plan.shape[1] - 2

    def turn(i, carry):
        first = i * per_turn
        most = jnp.clip(plan[step, group, first], 1, group)
        for count in range(1, group + 1):
            @pl.when(most == count)
            def _():
                for k in range(per_turn):
                    j = first + k
                    x = table[plan[step, 0, j]]
                    for g in range(1, count):
                        x = x + table[plan[step, g, j]]
                    put(plan[step, group + 1, j], x)

        return carry

    lax.fori_loop(0, plan.shape[2] // per_turn, turn, 0)


def clear_last(table):
    table[table.shape[0] - 1] = jnp.zeros(table.shape[1:], table.dtype)


def first_products_kernel(base, beside, across, passed, low, high, out, panel):
    _, d0, _ = place()
    choose(panel, [(d0 == 0, base), (d0 == 1, beside), (d0 == 2, across), (d0 == 3, passed)])
    products(panel, low, out, 0)
    products(panel, high, out, low.shape[0])
    clear_last(out)


def first_sums_kernel(per_turn, plan_in, table, out, plan, sem):
    pltpu.async_copy(plan_in, plan, sem).wait()

    def put(t, x):
        out[t] = x

    add_up(plan, 0, table, per_turn, put)


def half_products_kernel(base, beside, across, passed, across1, passed1, low, panel, table):
    odd, d0, d1 = place()
    plain = odd == 1
    choose(panel, [
        (d1 == 0, base),
        (jnp.logical_and(d1 == 1, plain) | jnp.logical_and(d0 == 0, ~plain), beside),
        (jnp.logical_and(d1 == 2, plain), across),
        (jnp.logical_and(d1 == 3, plain), passed),
        (jnp.logical_and(d0 == 2, ~plain), across1),
        (jnp.logical_and(d0 == 3, ~plain), passed1),
    ])
    products(panel, low, table, 0)
    clear_last(table)


def last_kernel(per_turn, plan_in, panel, high, summed, table_in, table, out, stage, plan, sem):
    del table_in
    planned = pltpu.make_async_copy(plan_in, plan, sem.at[0])
    planned.start()
    products(panel, high, table, panel.shape[0] - high.shape[0])
    planned.wait()

    def put(t, x):
        stage[t] = (summed[t] + x).astype(stage.dtype)
        pltpu.make_async_copy(stage.at[t], out.at[t], sem.at[1]).start()

    add_up(plan, 1, table, per_turn, put)
    pltpu.make_async_copy(stage, out, sem.at[1]).wait()


def cost(flops, bytes_accessed):
    return pl.CostEstimate(flops=flops, bytes_accessed=bytes_accessed, transcendentals=0)


def both_steps(left_blocks, right_blocks, left_index, right_index):
    row_count, col_count = lax.axis_size("row"), lax.axis_size("col")
    stored, block, _ = right_blocks.shape
    slots = left_index.shape[1]
    entries = stored * stored + 1
    both = ("row", "col")

    def permute(x, axis, pairs):
        return in_vmem(lax.ppermute(x, axis, pairs))

    left_at, right_at = left_index.transpose(0, 2, 1), right_index.transpose(0, 2, 1)
    base, low, high, plan = fetch(left_blocks, right_blocks, left_at, right_at, stored - stored // 4)
    bit = col_count // 2
    while bit > 2:
        pairs = full_pairs(row_count, col_count, lambda row: [
            (c, c ^ bit) for c in holders(row, col_count, 0, bit) | holders(row, col_count, 1, bit)
        ])
        base = merge(bit, base, lax.ppermute(base, both, pairs))
        bit //= 2
    crossing = full_pairs(row_count, col_count, lambda row: [
        (c, c ^ 2)
        for ahead in range(1 + row % 2)
        for c in holders(row, col_count, ahead, 2)
    ])
    again = full_pairs(row_count, col_count, lambda row: [
        (c, c ^ 2) for c in holders(row, col_count, 0, 2) if row % 2 == 0
    ])
    beside_pairs = [(c, c ^ 1) for c in range(col_count)]
    down = [(r, (r - 1) % row_count) for r in range(row_count)]
    base = in_vmem(base)
    across = permute(base, both, crossing)
    beside = permute(base, "col", beside_pairs)
    low1 = permute(low, "row", down)
    high1 = permute(high, "row", down)
    across1 = permute(beside, both, again)
    passed = permute(across, "col", beside_pairs)
    passed1 = permute(across1, "col", beside_pairs)

    plan = in_vmem(plan)
    per_turn = 8
    flops = 4 * stored * stored * block**3
    table_shape = jax.ShapeDtypeStruct((entries, block, block), jnp.float32)
    panel_shape = jax.ShapeDtypeStruct(base.shape, base.dtype)
    table = pl.pallas_call(
        first_products_kernel,
        out_shape=table_shape,
        in_specs=[VMEM] * 6,
        out_specs=VMEM,
        scratch_shapes=[pltpu.VMEM(base.shape, base.dtype)],
        compiler_params=pltpu.CompilerParams(vmem_limit_bytes=4 << 20),
        cost_estimate=cost(flops, 4 << 20),
        name="products",
    )(base, beside, across, passed, in_vmem(low), in_vmem(high))
    summed = pl.pallas_call(
        functools.partial(first_sums_kernel, per_turn),
        out_shape=jax.ShapeDtypeStruct((slots, block, block), jnp.float32),
        in_specs=[VMEM, VMEM],
        out_specs=VMEM,
        scratch_shapes=[pltpu.SMEM(plan.shape, plan.dtype), pltpu.SemaphoreType.DMA],
        compiler_params=pltpu.CompilerParams(vmem_limit_bytes=4 << 20),
        cost_estimate=cost(flops, 4 << 20),
        name="sums",
    )(plan, in_vmem(table))
    panel, table = pl.pallas_call(
        half_products_kernel,
        out_shape=(panel_shape, table_shape),
        in_specs=[VMEM] * 7,
        out_specs=(VMEM, VMEM),
        compiler_params=pltpu.CompilerParams(vmem_limit_bytes=4 << 20),
        cost_estimate=cost(flops // 2, 4 << 20),
        name="half",
    )(base, beside, across, passed, across1, passed1, low1)
    return pl.pallas_call(
        functools.partial(last_kernel, per_turn),
        out_shape=(table_shape, jax.ShapeDtypeStruct((slots, block, block), jnp.bfloat16)),
        in_specs=[VMEM] * 5,
        out_specs=(VMEM, HBM),
        scratch_shapes=[
            pltpu.VMEM((slots, block, block), jnp.bfloat16),
            pltpu.SMEM(plan.shape, plan.dtype),
            pltpu.SemaphoreType.DMA((2,)),
        ],
        input_output_aliases={4: 0},
        compiler_params=pltpu.CompilerParams(vmem_limit_bytes=6 << 20),
        cost_estimate=cost(2 * flops, 4 << 20),
        name="last",
    )(plan, in_vmem(panel), high1, in_vmem(summed), in_vmem(table))[1]


def solution(mesh):
    return jax.shard_map(
        both_steps,
        mesh=mesh,
        in_specs=(
            P(None, "row", "col", None),
            P("row", "col", None),
            P(None, "row", "col"),
            P(None, "row", "col"),
        ),
        out_specs=P("row", "col", None),
        check_vma=False,
    )
```

```python
import functools

import jax
import jax.numpy as jnp
from jax import lax
from jax.experimental import pallas as pl
from jax.experimental.pallas import tpu as pltpu
from jax.sharding import PartitionSpec as P


VMEM = pl.BlockSpec(memory_space=pltpu.VMEM)
HBM = pl.BlockSpec(memory_space=pltpu.HBM)


def in_vmem(x):
    return pltpu.with_memory_space_constraint(x, pltpu.VMEM)


def holders(row, col_count, ahead, bit):
    held = {(row + ahead) % col_count}
    step = col_count // 2
    while step > bit:
        held |= {c ^ step for c in held}
        step //= 2
    return held


def full_pairs(row_count, col_count, wanted):
    pairs = []
    for row in range(row_count):
        pair_of = dict(wanted(row))
        sources = [c for c in range(col_count) if c not in pair_of]
        targets = set(range(col_count)) - set(pair_of.values())
        for c in list(sources):
            if c ^ 1 in targets:
                pair_of[c] = c ^ 1
                targets.remove(c ^ 1)
                sources.remove(c)
        pair_of.update(zip(sources, sorted(targets)))
        pairs += [(row * col_count + c, row * col_count + to) for c, to in sorted(pair_of.items())]
    return pairs


def place():
    row, col = lax.axis_index("row"), lax.axis_index("col")
    return row % 2, (col ^ row) % 4, (col ^ (row + 1)) % 4


def plan_rows(index, dead):
    group, slots = index.shape
    rows = [index[g : g + 1] for g in range(group)]
    for turn in range(group):
        for g in range(turn % 2, group - 1, 2):
            rows[g], rows[g + 1] = jnp.minimum(*rows[g : g + 2]), jnp.maximum(*rows[g : g + 2])
    live = sum((row < dead).astype(jnp.float32) for row in rows)
    at_row = lax.broadcasted_iota(jnp.int32, (slots, slots), 0).astype(jnp.float32)
    at_col = lax.broadcasted_iota(jnp.int32, (slots, slots), 1).astype(jnp.float32)
    slot = at_col[:1]
    key = live * slots - slot
    column = jnp.sum(jnp.where(at_row == at_col, key, 0.0), axis=1, keepdims=True)
    rank = jnp.sum((key > column).astype(jnp.float32), axis=1, keepdims=True)
    pick = (rank == at_col).astype(jnp.float32)
    data = jnp.concatenate([row.astype(jnp.float32) for row in rows] + [live, slot], axis=0)
    sorted_data = jnp.dot(
        data, pick, precision=lax.Precision.HIGHEST, preferred_element_type=jnp.float32
    )
    return (sorted_data + 0.5).astype(jnp.int32)


def fetch_kernel(sizes, left, right, left_at, right_at, own, *rest):
    outs, (plan, at, sem) = rest[: len(sizes)], rest[len(sizes) :]
    row_count, col_count = lax.axis_size("row"), lax.axis_size("col")
    row = lax.axis_index("row")
    ahead = (row + lax.axis_index("col")) % 2
    slot = ((row + ahead) % row_count) // col_count
    stored = own.shape[0]
    pairs = [(left_at, at.at[0]), (right_at, at.at[1]), (left.at[slot], own)]
    for (source, first, count), out in zip(sizes, outs):
        origin = left.at[slot, pl.ds(first, count)] if source == 0 else right.at[pl.ds(first, count)]
        pairs.append((origin, out))
    copies = [pltpu.make_async_copy(x, y, sem.at[i]) for i, (x, y) in enumerate(pairs)]
    for copy in copies:
        copy.start()
    for copy in copies[:2]:
        copy.wait()
    dead = stored * stored
    index = jnp.where(at[0] < stored, at[1] * stored + at[0], dead)
    for step in range(plan.shape[0]):
        plan[step] = plan_rows(index[step], dead)
    for copy in copies[2:]:
        copy.wait()


def fetch(left_blocks, right_blocks, left_at, right_at, left_sizes, right_sizes):
    stored, *block = right_blocks.shape
    steps, group, slots = left_at.shape
    sizes = []
    for source, counts in ((0, left_sizes), (1, right_sizes)):
        first = 0
        for count in counts:
            sizes.append((source, first, count))
            first += count
    dtype = right_blocks.dtype
    outs = pl.pallas_call(
        functools.partial(fetch_kernel, tuple(sizes)),
        out_shape=(jax.ShapeDtypeStruct((stored, *block), dtype),)
        + tuple(jax.ShapeDtypeStruct((count, *block), dtype) for _, _, count in sizes)
        + (jax.ShapeDtypeStruct((steps, group + 2, slots), jnp.int32),),
        in_specs=[HBM] * 4,
        out_specs=(VMEM,) * (len(sizes) + 2),
        scratch_shapes=[
            pltpu.VMEM((2, steps, group, slots), jnp.int32),
            pltpu.SemaphoreType.DMA((len(sizes) + 3,)),
        ],
        compiler_params=pltpu.CompilerParams(vmem_limit_bytes=4 << 20),
        name="fetch",
    )(*(pltpu.with_memory_space_constraint(x, pltpu.HBM)
        for x in (left_blocks, right_blocks, left_at, right_at)))
    outs = [in_vmem(x) for x in outs]
    count = len(left_sizes)
    return outs[0], outs[1 : 1 + count], outs[1 + count : -1], outs[-1]


def cut_kernel(whole, *pieces):
    first = 0
    for piece in pieces:
        piece[...] = whole[pl.ds(first, piece.shape[0])]
        first += piece.shape[0]


def cut(whole, sizes):
    outs = pl.pallas_call(
        cut_kernel,
        out_shape=tuple(jax.ShapeDtypeStruct((n, *whole.shape[1:]), whole.dtype) for n in sizes),
        in_specs=[VMEM],
        out_specs=(VMEM,) * len(sizes),
        compiler_params=pltpu.CompilerParams(vmem_limit_bytes=4 << 20),
        name="cut",
    )(whole)
    return [in_vmem(x) for x in outs]


def merge_kernel(bit, base, received, out):
    row, col = lax.axis_index("row"), lax.axis_index("col")
    away = col ^ ((row + (row + col) % 2) % lax.axis_size("col"))
    take = (away & bit) != 0 if bit else row == lax.axis_size("row") - 1
    choose(out, [(take, received), (jnp.logical_not(take), base)])


def merge(bit, base, received):
    return in_vmem(pl.pallas_call(
        functools.partial(merge_kernel, bit),
        out_shape=jax.ShapeDtypeStruct(base.shape, base.dtype),
        in_specs=[VMEM, VMEM],
        out_specs=VMEM,
        compiler_params=pltpu.CompilerParams(vmem_limit_bytes=4 << 20),
        name="merge",
    )(in_vmem(base), in_vmem(received)))


def choose(panel, options):
    for condition, array in options:
        @pl.when(condition)
        def _():
            panel[...] = array[...]


def products(panel, right, out, first, span):
    stored, block, _ = panel.shape
    low, count = span
    rows = panel[pl.ds(low, count)].reshape(count * block, block)
    for q in range(right.shape[0] // 2):
        pair = jnp.concatenate([right[2 * q], right[2 * q + 1]], axis=1)
        x = jnp.dot(rows, pair, preferred_element_type=jnp.float32)
        base = (first + 2 * q) * stored + low
        out[pl.ds(base, count)] = x[:, :block].reshape(count, block, block)
        out[pl.ds(base + stored, count)] = x[:, block:].reshape(count, block, block)


def add_up(plan, step, table, per_turn, put):
    group = plan.shape[1] - 2

    def turn(i, carry):
        first = i * per_turn
        most = plan[step, group, first]

        def pick(low, high):
            if high - low == 1:
                for k in range(per_turn):
                    j = first + k
                    x = table[plan[step, 0, j]]
                    for g in range(1, low):
                        x = x + table[plan[step, g, j]]
                    put(plan[step, group + 1, j], x)
            else:
                middle = (low + high) // 2
                lax.cond(most < middle, lambda: pick(low, middle), lambda: pick(middle, high))

        pick(1, group + 1)
        return carry

    lax.fori_loop(0, plan.shape[2] // per_turn, turn, 0)


def clear_last(table):
    table[table.shape[0] - 1] = jnp.zeros(table.shape[1:], table.dtype)


def first_products_kernel(base, across, passed, beside0, beside1, right, panel, table):
    _, d0, _ = place()
    choose(panel, [(d0 == 0, base), (d0 == 2, across), (d0 == 3, passed)])

    @pl.when(d0 == 1)
    def _():
        low = beside0.shape[0]
        panel[pl.ds(0, low)] = beside0[...]
        panel[pl.ds(low, beside1.shape[0])] = beside1[...]

    products(panel, right, table, 0, (0, panel.shape[0]))
    clear_last(table)


def finish(plan_in, plan, sem, panel, right, table):
    planned = pltpu.make_async_copy(plan_in, plan, sem)
    planned.start()
    stored = panel.shape[0]
    products(panel, right, table, stored - right.shape[0], (0, stored))
    planned.wait()


def first_sums_kernel(per_turn, plan_in, panel, right, table_in, table, out, plan, sem):
    del table_in
    finish(plan_in, plan, sem, panel, right, table)

    def put(t, x):
        out[t] = x

    add_up(plan, 0, table, per_turn, put)


def choose_second(panel, span, base, beside, across, passed, across1, passed1):
    odd, d0, d1 = place()
    plain = odd == 1
    low, count = span
    part = pl.ds(low, count)
    choose(panel.at[part], [
        (d1 == 0, base.at[part]),
        (jnp.logical_and(d1 == 1, plain) | jnp.logical_and(d0 == 0, ~plain), beside),
        (jnp.logical_and(d1 == 2, plain), across.at[part]),
        (jnp.logical_and(d1 == 3, plain), passed.at[part]),
        (jnp.logical_and(d0 == 2, ~plain), across1),
        (jnp.logical_and(d0 == 3, ~plain), passed1),
    ])


def second_products_kernel(base, across, passed, beside, across1, passed1, right, panel, table):
    span = 0, beside.shape[0]
    choose_second(panel, span, base, beside, across, passed, across1, passed1)
    products(panel, right, table, 0, span)
    clear_last(table)


def middle_kernel(
    base, across, passed, beside, across1, passed1, right, panel_in, table_in, panel, table
):
    del panel_in, table_in
    span = panel.shape[0] - beside.shape[0], beside.shape[0]
    choose_second(panel, span, base, beside, across, passed, across1, passed1)
    products(panel, right, table, 0, span)


def last_kernel(per_turn, plan_in, panel, right, summed, table_in, table, out, stage, plan, sem):
    del table_in
    finish(plan_in, plan, sem.at[0], panel, right, table)

    def put(t, x):
        stage[t] = (summed[t] + x).astype(stage.dtype)
        pltpu.make_async_copy(stage.at[t], out.at[t], sem.at[1]).start()

    add_up(plan, 1, table, per_turn, put)
    pltpu.make_async_copy(stage, out, sem.at[1]).wait()


def cost(flops, bytes_accessed):
    return pl.CostEstimate(flops=flops, bytes_accessed=bytes_accessed, transcendentals=0)


def both_steps(left_blocks, right_blocks, left_index, right_index):
    row_count, col_count = lax.axis_size("row"), lax.axis_size("col")
    stored, block, _ = right_blocks.shape
    slots = left_index.shape[1]
    entries = stored * stored + 1
    both = ("row", "col")
    left_sizes = (stored - stored // 4, stored // 4)
    right_sizes = (stored - stored // 4, stored // 4)

    def permute(x, axis, pairs):
        return in_vmem(lax.ppermute(x, axis, pairs))

    left_at, right_at = left_index.transpose(0, 2, 1), right_index.transpose(0, 2, 1)
    base, pieces, rights, plan = fetch(
        left_blocks, right_blocks, left_at, right_at, left_sizes, right_sizes
    )
    bit = col_count // 2
    spread = bit > 2
    while bit > 2:
        pairs = full_pairs(row_count, col_count, lambda row: [
            (c, c ^ bit) for c in holders(row, col_count, 0, bit) | holders(row, col_count, 1, bit)
        ])
        base = merge(bit, base, lax.ppermute(base, both, pairs))
        bit //= 2
    if spread:
        pieces = cut(base, left_sizes)

    def crossing(rows, panels):
        return full_pairs(row_count, col_count, lambda row: [
            (c, c ^ 2)
            for ahead in range(panels(row))
            for c in holders(row, col_count, ahead, 2)
            if row in rows
        ])

    near = [(c, c ^ 1) for c in range(col_count)]
    down = [(r, (r - 1) % row_count) for r in range(row_count)]
    rows = range(row_count)
    cross = permute(base, both, crossing(rows[:-1], lambda row: 1 + row % 2))
    besides = [permute(x, "col", near) for x in pieces]
    moved = [permute(x, "row", down) for x in rights]
    last_cross = permute(base, both, crossing(rows[-1:], lambda row: 1 + row % 2))
    across1 = [permute(x, both, crossing(rows[::2], lambda row: 1)) for x in besides]
    across = merge(0, cross, last_cross)
    passed = permute(across, "col", near)
    passed1 = [permute(x, "col", near) for x in across1]

    per_turn = min(slots, 16)
    flops = 4 * stored * stored * block**3
    table_shape = jax.ShapeDtypeStruct((entries, block, block), jnp.float32)
    panel_shape = jax.ShapeDtypeStruct(base.shape, base.dtype)
    plan_scratch = pltpu.SMEM(plan.shape, plan.dtype)
    small = pltpu.CompilerParams(vmem_limit_bytes=6 << 20)
    panel, table = pl.pallas_call(
        first_products_kernel,
        out_shape=(panel_shape, table_shape),
        in_specs=[VMEM] * 6,
        out_specs=(VMEM, VMEM),
        compiler_params=small,
        cost_estimate=cost(flops, 4 << 20),
        name="products",
    )(base, across, passed, *besides, rights[0])
    _, summed = pl.pallas_call(
        functools.partial(first_sums_kernel, per_turn),
        out_shape=(table_shape, jax.ShapeDtypeStruct((slots, block, block), jnp.float32)),
        in_specs=[VMEM] * 4,
        out_specs=(VMEM, VMEM),
        scratch_shapes=[plan_scratch, pltpu.SemaphoreType.DMA],
        input_output_aliases={3: 0},
        compiler_params=small,
        cost_estimate=cost(flops, 4 << 20),
        name="sums",
    )(plan, in_vmem(panel), rights[1], in_vmem(table))
    panel, table = pl.pallas_call(
        second_products_kernel,
        out_shape=(panel_shape, table_shape),
        in_specs=[VMEM] * 7,
        out_specs=(VMEM, VMEM),
        compiler_params=small,
        cost_estimate=cost(flops // 2, 4 << 20),
        name="second",
    )(base, across, passed, besides[0], across1[0], passed1[0], moved[0])
    panel, table = pl.pallas_call(
        middle_kernel,
        out_shape=(panel_shape, table_shape),
        in_specs=[VMEM] * 9,
        out_specs=(VMEM, VMEM),
        input_output_aliases={7: 0, 8: 1},
        compiler_params=small,
        cost_estimate=cost(flops, 4 << 20),
        name="middle",
    )(
        base, across, passed, besides[1], across1[1], passed1[1], moved[0],
        in_vmem(panel), in_vmem(table),
    )
    return pl.pallas_call(
        functools.partial(last_kernel, per_turn),
        out_shape=(table_shape, jax.ShapeDtypeStruct((slots, block, block), jnp.bfloat16)),
        in_specs=[VMEM] * 5,
        out_specs=(VMEM, HBM),
        scratch_shapes=[
            pltpu.VMEM((slots, block, block), jnp.bfloat16),
            plan_scratch,
            pltpu.SemaphoreType.DMA((2,)),
        ],
        input_output_aliases={4: 0},
        compiler_params=small,
        cost_estimate=cost(2 * flops, 4 << 20),
        name="last",
    )(plan, in_vmem(panel), moved[1], in_vmem(summed), in_vmem(table))[1]


def solution(mesh):
    return jax.shard_map(
        both_steps,
        mesh=mesh,
        in_specs=(
            P(None, "row", "col", None),
            P("row", "col", None),
            P(None, "row", "col"),
            P(None, "row", "col"),
        ),
        out_specs=P("row", "col", None),
        check_vma=False,
    )
```

```python
import functools

import jax
import jax.numpy as jnp
from jax import lax
from jax.experimental import pallas as pl
from jax.experimental.pallas import tpu as pltpu
from jax.sharding import PartitionSpec as P


VMEM = pl.BlockSpec(memory_space=pltpu.VMEM)
HBM = pl.BlockSpec(memory_space=pltpu.HBM)


def in_vmem(x):
    return pltpu.with_memory_space_constraint(x, pltpu.VMEM)


def holders(row, col_count, ahead, bit):
    held = {(row + ahead) % col_count}
    step = col_count // 2
    while step > bit:
        held |= {c ^ step for c in held}
        step //= 2
    return held


def full_pairs(row_count, col_count, wanted):
    pairs = []
    for row in range(row_count):
        pair_of = dict(wanted(row))
        sources = [c for c in range(col_count) if c not in pair_of]
        targets = set(range(col_count)) - set(pair_of.values())
        for c in list(sources):
            if c ^ 1 in targets:
                pair_of[c] = c ^ 1
                targets.remove(c ^ 1)
                sources.remove(c)
        pair_of.update(zip(sources, sorted(targets)))
        pairs += [(row * col_count + c, row * col_count + to) for c, to in sorted(pair_of.items())]
    return pairs


def place():
    row, col = lax.axis_index("row"), lax.axis_index("col")
    return row % 2, (col ^ row) % 4, (col ^ (row + 1)) % 4


def plan_rows(index, dead):
    group, slots = index.shape
    rows = [index[g : g + 1] for g in range(group)]
    for turn in range(group):
        for g in range(turn % 2, group - 1, 2):
            rows[g], rows[g + 1] = jnp.minimum(*rows[g : g + 2]), jnp.maximum(*rows[g : g + 2])
    live = sum((row < dead).astype(jnp.float32) for row in rows)
    at_row = lax.broadcasted_iota(jnp.int32, (slots, slots), 0).astype(jnp.float32)
    at_col = lax.broadcasted_iota(jnp.int32, (slots, slots), 1).astype(jnp.float32)
    slot = at_col[:1]
    key = live * slots - slot
    column = jnp.sum(jnp.where(at_row == at_col, key, 0.0), axis=1, keepdims=True)
    rank = jnp.sum((key > column).astype(jnp.float32), axis=1, keepdims=True)
    pick = (rank == at_col).astype(jnp.float32)
    data = jnp.concatenate([row.astype(jnp.float32) for row in rows] + [live, slot], axis=0)
    sorted_data = jnp.dot(
        data, pick, precision=lax.Precision.HIGHEST, preferred_element_type=jnp.float32
    )
    return (sorted_data + 0.5).astype(jnp.int32)


def fetch_kernel(sizes, stored, left, right, left_at, right_at, *rest):
    outs, (plan, at, sem) = rest[: len(sizes)], rest[len(sizes) :]
    row_count, col_count = lax.axis_size("row"), lax.axis_size("col")
    row = lax.axis_index("row")
    ahead = (row + lax.axis_index("col")) % 2
    slot = ((row + ahead) % row_count) // col_count
    pairs = [(left_at, at.at[0]), (right_at, at.at[1])]
    for (source, first, count), out in zip(sizes, outs):
        origin = left.at[slot, pl.ds(first, count)] if source == 0 else right.at[pl.ds(first, count)]
        pairs.append((origin, out))
    copies = [pltpu.make_async_copy(x, y, sem.at[i]) for i, (x, y) in enumerate(pairs)]
    for copy in copies:
        copy.start()
    for copy in copies[:2]:
        copy.wait()
    dead = stored * stored
    index = jnp.where(at[0] < stored, at[1] * stored + at[0], dead)
    for step in range(plan.shape[0]):
        plan[step] = plan_rows(index[step], dead)
    for copy in copies[2:]:
        copy.wait()


def fetch(left_blocks, right_blocks, left_at, right_at, left_sizes, right_sizes):
    stored, *block = right_blocks.shape
    steps, group, slots = left_at.shape
    sizes = []
    for source, counts in ((0, left_sizes), (1, right_sizes)):
        first = 0
        for count in counts:
            sizes.append((source, first, count))
            first += count
    dtype = right_blocks.dtype
    outs = pl.pallas_call(
        functools.partial(fetch_kernel, tuple(sizes), stored),
        out_shape=tuple(jax.ShapeDtypeStruct((count, *block), dtype) for _, _, count in sizes)
        + (jax.ShapeDtypeStruct((steps, group + 2, slots), jnp.int32),),
        in_specs=[HBM] * 4,
        out_specs=(VMEM,) * (len(sizes) + 1),
        scratch_shapes=[
            pltpu.VMEM((2, steps, group, slots), jnp.int32),
            pltpu.SemaphoreType.DMA((len(sizes) + 2,)),
        ],
        compiler_params=pltpu.CompilerParams(vmem_limit_bytes=4 << 20),
        name="fetch",
    )(*(pltpu.with_memory_space_constraint(x, pltpu.HBM)
        for x in (left_blocks, right_blocks, left_at, right_at)))
    outs = [in_vmem(x) for x in outs]
    count = len(left_sizes)
    return outs[:count], outs[count:-1], outs[-1]


def merge_kernel(bit, base, received, out):
    row, col = lax.axis_index("row"), lax.axis_index("col")
    away = col ^ ((row + (row + col) % 2) % lax.axis_size("col"))
    take = (away & bit) != 0 if bit else row == lax.axis_size("row") - 1
    choose(out, [(take, received), (jnp.logical_not(take), base)])


def merge(bit, base, received):
    return in_vmem(pl.pallas_call(
        functools.partial(merge_kernel, bit),
        out_shape=jax.ShapeDtypeStruct(base.shape, base.dtype),
        in_specs=[VMEM, VMEM],
        out_specs=VMEM,
        compiler_params=pltpu.CompilerParams(vmem_limit_bytes=4 << 20),
        name="merge",
    )(in_vmem(base), in_vmem(received)))


def choose(panel, options):
    for condition, array in options:
        @pl.when(condition)
        def _():
            panel[...] = array[...]


def products(panel, right, out, first, span):
    stored, block, _ = panel.shape
    low, count = span
    rows = panel[pl.ds(low, count)].reshape(count * block, block)
    for q in range(right.shape[0] // 2):
        pair = jnp.concatenate([right[2 * q], right[2 * q + 1]], axis=1)
        x = jnp.dot(rows, pair, preferred_element_type=jnp.float32)
        base = (first + 2 * q) * stored + low
        out[pl.ds(base, count)] = x[:, :block].reshape(count, block, block)
        out[pl.ds(base + stored, count)] = x[:, block:].reshape(count, block, block)


def add_up(plan, table, per_turn, put):
    group, slots = plan.shape[0] - 2, plan.shape[1]

    def turn(i, carry):
        first = slots - (i + 1) * per_turn
        most = plan[group, first]

        def pick(low, high):
            if high - low == 1:
                for k in range(per_turn):
                    j = first + k
                    x = table[plan[0, j]]
                    for g in range(1, low):
                        x = x + table[plan[g, j]]
                    put(plan[group + 1, j], x)
            else:
                middle = (low + high) // 2
                lax.cond(most < middle, lambda: pick(low, middle), lambda: pick(middle, high))

        pick(1, group + 1)
        return carry

    lax.fori_loop(0, slots // per_turn, turn, 0)


def clear_last(table):
    table[table.shape[0] - 1] = jnp.zeros(table.shape[1:], table.dtype)


def piece_kernel(step, first, started, base, beside, across, passed, *rest):
    *later, right, panel, table = rest[:-4] + rest[-2:] if started else rest
    extra = None
    if step == 0 and started:
        (right,), extra = later, right
    odd, d0, d1 = place()
    part = panel.at[pl.ds(first, base.shape[0])]
    if step == 0:
        choose(part, [(d0 == 0, base), (d0 == 1, beside), (d0 == 2, across), (d0 == 3, passed)])
    else:
        across1, passed1 = later
        plain = odd == 1
        choose(part, [
            (d1 == 0, base),
            (jnp.logical_and(d1 == 1, plain) | jnp.logical_and(d0 == 0, ~plain), beside),
            (jnp.logical_and(d1 == 2, plain), across),
            (jnp.logical_and(d1 == 3, plain), passed),
            (jnp.logical_and(d0 == 2, ~plain), across1),
            (jnp.logical_and(d0 == 3, ~plain), passed1),
        ])
    products(panel, right, table, 0, (first, base.shape[0]))
    if extra is not None:
        products(panel, extra, table, right.shape[0], (0, first))
    if not started:
        clear_last(table)


def finish(plan_in, plan, sem, panel, right, table, span):
    planned = pltpu.make_async_copy(plan_in, plan, sem)
    planned.start()
    products(panel, right, table, panel.shape[0] - right.shape[0], span)
    planned.wait()


def first_sums_kernel(per_turn, first, plan_in, panel, right, table_in, table, out, plan, sem):
    del table_in
    finish(plan_in.at[0], plan, sem, panel, right, table, (first, panel.shape[0] - first))

    def put(t, x):
        out[t] = x

    add_up(plan, table, per_turn, put)


def last_kernel(per_turn, plan_in, panel, right, summed, table_in, table, out, stage, plan, sem):
    del table_in
    finish(plan_in.at[1], plan, sem.at[0], panel, right, table, (0, panel.shape[0]))

    def put(t, x):
        stage[t] = (summed[t] + x).astype(stage.dtype)
        pltpu.make_async_copy(stage.at[t], out.at[t], sem.at[1]).start()

    add_up(plan, table, per_turn, put)
    pltpu.make_async_copy(stage, out, sem.at[1]).wait()


def cost(flops, bytes_accessed):
    return pl.CostEstimate(flops=flops, bytes_accessed=bytes_accessed, transcendentals=0)


def both_steps(left_blocks, right_blocks, left_index, right_index):
    row_count, col_count = lax.axis_size("row"), lax.axis_size("col")
    stored, block, _ = right_blocks.shape
    slots = left_index.shape[1]
    entries = stored * stored + 1
    both = ("row", "col")
    left_sizes = (stored - 3 * stored // 8, 3 * stored // 8)
    right_sizes = (stored - 3 * stored // 8, 3 * stored // 8)

    def permute(x, axis, pairs):
        return in_vmem(lax.ppermute(x, axis, pairs))

    left_at, right_at = left_index.transpose(0, 2, 1), right_index.transpose(0, 2, 1)
    pieces, rights, plan = fetch(
        left_blocks, right_blocks, left_at, right_at, left_sizes, right_sizes
    )
    bit = col_count // 2
    while bit > 2:
        pairs = full_pairs(row_count, col_count, lambda row: [
            (c, c ^ bit) for c in holders(row, col_count, 0, bit) | holders(row, col_count, 1, bit)
        ])
        pieces = [merge(bit, x, lax.ppermute(x, both, pairs)) for x in pieces]
        bit //= 2

    def crossing(rows, panels):
        return full_pairs(row_count, col_count, lambda row: [
            (c, c ^ 2)
            for ahead in range(panels(row))
            for c in holders(row, col_count, ahead, 2)
            if row in rows
        ])

    near = [(c, c ^ 1) for c in range(col_count)]
    down = [(r, (r - 1) % row_count) for r in range(row_count)]
    rows = range(row_count)
    first_rows = crossing(rows[:-1], lambda row: 1 + row % 2)
    last_row = crossing(rows[-1:], lambda row: 1 + row % 2)
    even_rows = crossing(rows[::2], lambda row: 1)
    cross = [permute(x, both, first_rows) for x in pieces]
    beside = [permute(x, "col", near) for x in pieces]
    moved = [permute(x, "row", down) for x in rights]
    last_cross = [permute(x, both, last_row) for x in pieces]
    across1 = [permute(x, both, even_rows) for x in beside]
    across = [merge(0, x, y) for x, y in zip(cross, last_cross)]
    passed = [permute(x, "col", near) for x in across]
    passed1 = [permute(x, "col", near) for x in across1]

    per_turn = min(slots, 16)
    flops = 4 * stored * stored * block**3
    table_shape = jax.ShapeDtypeStruct((entries, block, block), jnp.float32)
    panel_shape = jax.ShapeDtypeStruct(right_blocks.shape, right_blocks.dtype)
    plan_scratch = pltpu.SMEM(plan.shape[1:], plan.dtype)
    small = pltpu.CompilerParams(vmem_limit_bytes=6 << 20)

    def step_products(step, right):
        state = ()
        first = 0
        for i, base in enumerate(pieces):
            sources = (base, beside[i], across[i], passed[i])
            if step == 1:
                sources += (across1[i], passed1[i])
            if step == 0 and i:
                sources += (right, rights[1])
            else:
                sources += (right,)
            operands = sources + state
            state = pl.pallas_call(
                functools.partial(piece_kernel, step, first, i > 0),
                out_shape=(panel_shape, table_shape),
                in_specs=[VMEM] * len(operands),
                out_specs=(VMEM, VMEM),
                input_output_aliases={len(operands) - 2: 0, len(operands) - 1: 1} if i else {},
                compiler_params=small,
                cost_estimate=cost(flops, 4 << 20),
            )(*operands)
            state = tuple(map(in_vmem, state))
            first += base.shape[0]
        return state

    panel, table = step_products(0, rights[0])
    _, summed = pl.pallas_call(
        functools.partial(first_sums_kernel, per_turn, left_sizes[0]),
        out_shape=(table_shape, jax.ShapeDtypeStruct((slots, block, block), jnp.float32)),
        in_specs=[VMEM] * 4,
        out_specs=(VMEM, VMEM),
        scratch_shapes=[plan_scratch, pltpu.SemaphoreType.DMA],
        input_output_aliases={3: 0},
        compiler_params=small,
        cost_estimate=cost(flops, 4 << 20),
        name="sums",
    )(plan, panel, rights[1], table)
    panel, table = step_products(1, moved[0])
    return pl.pallas_call(
        functools.partial(last_kernel, per_turn),
        out_shape=(table_shape, jax.ShapeDtypeStruct((slots, block, block), jnp.bfloat16)),
        in_specs=[VMEM] * 5,
        out_specs=(VMEM, HBM),
        scratch_shapes=[
            pltpu.VMEM((slots, block, block), jnp.bfloat16),
            plan_scratch,
            pltpu.SemaphoreType.DMA((2,)),
        ],
        input_output_aliases={4: 0},
        compiler_params=small,
        cost_estimate=cost(2 * flops, 4 << 20),
        name="last",
    )(plan, panel, moved[1], in_vmem(summed), table)[1]


def solution(mesh):
    return jax.shard_map(
        both_steps,
        mesh=mesh,
        in_specs=(
            P(None, "row", "col", None),
            P("row", "col", None),
            P(None, "row", "col"),
            P(None, "row", "col"),
        ),
        out_specs=P("row", "col", None),
        check_vma=False,
    )
```
